768 devices in a mesh: ctx: 192 (over z, y_hi, x, core), dp: 4 (over y_lo).
Axes of the slice: x: 4, y: 8 (y_hi: 2, y_lo: 4; y = y_hi * 4 + y_lo), z: 12, core: 2. Of those that a mesh axis runs over, the one named last changes fastest.
Arguments:
- queries: bfloat16 [98304, 4096], P(('dp', 'ctx')), parts along dimension 0, may hold values from -16 to 16
- key_rows: bfloat16 [98304, 4096], P(('dp', 'ctx')), parts along dimension 0, may hold values from -16 to 16
- value_rows: bfloat16 [98304, 4096], P(('dp', 'ctx')), parts along dimension 0, may hold values from -6 to 6
- lengths: int32 [512], P('dp'), parts along dimension 0, may hold values from 1 to 256, 24576 in all
- norm_gain: float32 [4096], replicated, may hold values from 0.1 to 1.9
- filters: bfloat16 [256, 128], replicated, may hold values from -0.5 to 0.5
- bypass: float32 [4096], replicated, may hold values from -4 to 4
Outputs:
- mixed: bfloat16 [98304, 4096], P(('dp', 'ctx')), parts along dimension 0
The draws below stay inside these ranges and needn't reach their ends.
There are 4 independent parts, one for each index of `dp`. The reference program is written for one: setup_inputs(seed, part) draws one part's arguments, and reference() takes and returns one part's arrays. A program takes and returns all parts, laid end to end along the dimension named above; an argument that names none is the same for every part. Nothing has to cross between parts.
Inputs may be any that keep to these rules, and one draw needn't show every extreme that they name: The lengths sum to 24576; one of them is exactly 256.
All inputs are finite; a program needn't handle non-finite values.
Results may differ from the reference program's by a relative error of at most 0.012.
Values may be sent and summed in bfloat16 or wider, within the bound.
A program may use at most 32 MiB of HBM per device.

```python
import math
import jax
import jax.numpy as jnp
import numpy as np
from jax import lax

TOK_DEV = 128
HEADS = 32
HEAD_DIM = 128
TAPS = 128
CHANNELS = 4096
GROUPS = 256
DOC_MOST = 256
SEQ = 24576
NDOCS = 128


def draw_queries(key, part):
    drawn = jnp.clip(jax.random.normal(jax.random.fold_in(key, 1), (SEQ, HEADS * HEAD_DIM), jnp.float32), -6.0, 6.0)
    return drawn.astype(jnp.bfloat16)


def draw_key_rows(key, part):
    drawn = jnp.clip(jax.random.normal(jax.random.fold_in(key, 2), (SEQ, HEADS * HEAD_DIM), jnp.float32), -6.0, 6.0)
    return drawn.astype(jnp.bfloat16)


def shard_levels(rng, shape, cuts, low, top_value):
    factor_of = 1.0
    for dim, shards_of in cuts:
        steps = jax.random.uniform(jax.random.fold_in(jax.random.fold_in(rng, 6), dim), (shards_of,), jnp.float32, low / len(cuts), top_value / len(cuts))
        factor_of = factor_of * jnp.repeat(jnp.exp(steps), shape[dim] // shards_of).reshape((-1,) + (1,) * (len(shape) - 1 - dim))
    return factor_of


def length_profile(count, total, bound, skew):
    portions = [(1 << 20) // math.isqrt(grade ** skew) + 1 for grade in range(2, count + 1)]
    rest, holding = total - bound - (count - 1), [1] * (count - 1)
    while rest > 0:
        candidates = [i for i in range(count - 1) if holding[i] < bound]
        pool, budget = sum([portions[i] for i in candidates]), rest
        for i in candidates:
            more = min(bound - holding[i], max(1, budget * portions[i] // pool), rest)
            holding[i] = holding[i] + more
            rest = rest - more
    return np.array([bound] + holding)


def uneven_parts(key, number_of, total, most, lean):
    if number_of == 2:
        one = jax.random.randint(key, (), max(1, total - most), min(most, total - 1) + 1)
        return jnp.stack([one, total - one])
    sizes = jnp.asarray(length_profile(number_of, total, most, lean), jnp.int32)
    pairs = (number_of - 1) // 2
    donor, taker = sizes[1:1 + 2 * pairs:2], sizes[2:2 + 2 * pairs:2]
    slack = jnp.minimum(donor - 1, most - taker)
    moved = jax.random.randint(jax.random.fold_in(key, 1), (pairs,), 0, 1 << 20) % (slack + 1)
    sizes = sizes.at[1:1 + 2 * pairs:2].set(donor - moved).at[2:2 + 2 * pairs:2].set(taker + moved)
    return sizes[jax.random.permutation(jax.random.fold_in(key, 2), number_of)]


def normal_values(rng, dims, scale, reach, shards=(), kind=jnp.bfloat16):
    array = jax.random.normal(rng, dims, jnp.float32) * scale
    if len(shards) > 0:
        array = shard_levels(rng, dims, shards, -0.22, 0.18) * array
    return jnp.clip(array, min=-reach, max=reach).astype(kind)


def setup_inputs(seed: int = 0, part: int = 0) -> dict:
    arg_keys = jax.random.split(jax.random.key(seed), 8)
    part_splits = jax.random.split(jax.random.fold_in(arg_keys[7], part), 8)
    queries = draw_queries(jax.random.fold_in(jax.random.fold_in(arg_keys[7], part), 71), part)
    key_rows = draw_key_rows(jax.random.fold_in(jax.random.fold_in(arg_keys[7], part), 71), part)
    value_rows = normal_values(part_splits[2], (SEQ, CHANNELS), 1.0, 6.0, ((0, 192),))
    lengths = uneven_parts(part_splits[3], NDOCS, SEQ, DOC_MOST, 2).astype(jnp.int32)
    norm_gain = jnp.clip(1.0 + 0.18 * jax.random.normal(arg_keys[4], (CHANNELS,), jnp.float32), 0.1, 1.9)
    filters = normal_values(arg_keys[5], (GROUPS, TAPS), TAPS ** -0.5, 0.5)
    bypass = normal_values(arg_keys[6], (CHANNELS,), 1.0, 4.0, (), jnp.float32)
    return {"queries": queries, "key_rows": key_rows, "value_rows": value_rows, "lengths": lengths, "norm_gain": norm_gain, "filters": filters, "bypass": bypass}


def starts_of(lengths, count):
    ends = jnp.cumsum(lengths).astype(jnp.int32)
    position = jnp.arange(count, dtype=jnp.int32)
    passed = ends[None, :] <= position[:, None]
    return lax.optimization_barrier(jnp.sum(jnp.where(passed, lengths[None, :], 0), axis=1)).astype(jnp.int32)

def reference(queries, key_rows, value_rows, lengths, norm_gain, filters, bypass):
    seq_len = queries.shape[0]
    width = queries.shape[1]
    heads = width // HEAD_DIM
    starts = starts_of(lengths, seq_len)
    key_padded = jnp.concatenate([jnp.zeros((DOC_MOST, width), key_rows.dtype), key_rows], axis=0)
    value_padded = jnp.concatenate([jnp.zeros((DOC_MOST, width), value_rows.dtype), value_rows], axis=0)
    scale = 1.0 / math.sqrt(HEAD_DIM)

    def attend_block(block):
        begin = (block * TOK_DEV).astype(jnp.int32)
        query_part = lax.dynamic_slice_in_dim(queries, begin, TOK_DEV, 0).astype(jnp.float32)
        key_part = lax.dynamic_slice_in_dim(key_padded, begin, TOK_DEV + DOC_MOST, 0).astype(jnp.float32)
        value_part = lax.dynamic_slice_in_dim(value_padded, begin, TOK_DEV + DOC_MOST, 0).astype(jnp.float32)
        start_part = lax.dynamic_slice_in_dim(starts, begin, TOK_DEV, 0)
        query_heads = query_part.reshape(TOK_DEV, heads, HEAD_DIM)
        key_heads = key_part.reshape(TOK_DEV + DOC_MOST, heads, HEAD_DIM)
        value_heads = value_part.reshape(TOK_DEV + DOC_MOST, heads, HEAD_DIM)
        scores = jnp.einsum('thd,uhd->htu', query_heads, key_heads) * scale
        query_pos = begin + jnp.arange(TOK_DEV, dtype=jnp.int32)
        key_pos = begin - DOC_MOST + jnp.arange(TOK_DEV + DOC_MOST, dtype=jnp.int32)
        valid = (key_pos[None, :] >= start_part[:, None]) & (key_pos[None, :] <= query_pos[:, None])
        scores = jnp.where(valid[None], scores, jnp.float32(-1e+30))
        top = lax.optimization_barrier(jnp.max(scores, axis=2, keepdims=True))
        raised = jnp.where(valid[None], jnp.exp(scores - top), jnp.float32(0.0))
        weights = (raised / lax.optimization_barrier(jnp.sum(raised, axis=2, keepdims=True))).astype(jnp.bfloat16)
        result = jnp.einsum('htu,uhd->thd', weights.astype(jnp.float32), value_heads)
        return result.astype(jnp.bfloat16).reshape(TOK_DEV, width)
    blocks = seq_len // TOK_DEV
    attended = lax.map(attend_block, jnp.arange(blocks, dtype=jnp.int32)).reshape(seq_len, width)
    attended32 = attended.astype(jnp.float32)
    squares = lax.optimization_barrier(jnp.mean(attended32 * attended32, axis=1, keepdims=True))
    normed = (attended32 * lax.rsqrt(squares + 1e-06) * norm_gain[None, :]).astype(jnp.bfloat16)
    normed32 = normed.astype(jnp.float32)
    group_size = width // filters.shape[0]
    channel_filters = jnp.repeat(filters.astype(jnp.float32), group_size, axis=0).T
    normed_padded = jnp.concatenate([jnp.zeros((TAPS - 1, width), jnp.float32), normed32], axis=0)

    def conv_block(block):
        begin = (block * TOK_DEV).astype(jnp.int32)
        window = lax.dynamic_slice_in_dim(normed_padded, begin, TOK_DEV + TAPS - 1, 0)
        position = begin + jnp.arange(TOK_DEV, dtype=jnp.int32)
        start_part = lax.dynamic_slice_in_dim(starts, begin, TOK_DEV, 0)

        def add_tap(tap, total):
            tap = jnp.asarray(tap).astype(jnp.int32)
            offset = (TAPS - 1 - tap).astype(jnp.int32)
            piece = lax.dynamic_slice_in_dim(window, offset, TOK_DEV, 0)
            coeff = lax.dynamic_slice_in_dim(channel_filters, tap, 1, 0)
            allowed = (position - tap >= start_part)[:, None]
            return total + jnp.where(allowed, piece * coeff, jnp.float32(0.0))
        return lax.fori_loop(0, TAPS, add_tap, jnp.zeros((TOK_DEV, width), jnp.float32))
    convolved = lax.map(conv_block, jnp.arange(blocks, dtype=jnp.int32)).reshape(seq_len, width)
    return (convolved + bypass[None, :] * normed32).astype(jnp.bfloat16)
```

```python
import functools
import math

import jax
import jax.numpy as jnp
from jax import lax
from jax.experimental import pallas as pl
from jax.experimental.pallas import tpu as pltpu
from jax.sharding import PartitionSpec as P

HEAD_DIM = 128
ROWS = 128
TAPS = 128
GROUP = 16
LANES = 128
F32 = jnp.float32
BF16 = jnp.bfloat16
EXPONENT = math.log2(math.e) / math.sqrt(HEAD_DIM)
MASKED = -1e30


def passed_along(x, axis, by):
    length = lax.axis_size(axis)
    pairs = [(i, i + by) for i in range(length) if 0 <= i + by < length]
    return lax.ppermute(x, axis, pairs)


def row_starts(lengths_row, first_row):
    docs = lengths_row.shape[1]
    upto = (
        lax.broadcasted_iota(jnp.int32, (docs, docs), 0) <= lax.broadcasted_iota(jnp.int32, (docs, docs), 1)
    ).astype(F32)
    sizes = jnp.broadcast_to(lengths_row.astype(F32), (8, docs))
    ends = jnp.dot(sizes.astype(BF16), upto.astype(BF16), preferred_element_type=F32)
    position = (first_row + lax.broadcasted_iota(jnp.int32, (ROWS, docs), 0)).astype(F32)
    passed = jnp.broadcast_to(ends[0:1], (ROWS, docs)) <= position
    return jnp.sum(jnp.where(passed, jnp.broadcast_to(sizes[0:1], (ROWS, docs)), 0.0), axis=1, keepdims=True)


def key_bias(starts, first_row, key_first, span):
    query_pos = (first_row + lax.broadcasted_iota(jnp.int32, (ROWS, span), 0)).astype(F32)
    key_pos = (key_first + lax.broadcasted_iota(jnp.int32, (ROWS, span), 1)).astype(F32)
    valid = (key_pos >= starts) & (key_pos <= query_pos)
    return jnp.where(valid, 0.0, MASKED)


def attend_head(query, keys, values, bias):
    scores = lax.dot_general(query, keys, (((1,), (1,)), ((), ())), preferred_element_type=F32) + bias
    top = jnp.max(scores, axis=1, keepdims=True)
    raised = jnp.exp2((scores - top) * EXPONENT)
    total = jnp.sum(raised, axis=1, keepdims=True)
    mixed = jnp.dot(raised.astype(BF16), values, preferred_element_type=F32)
    return mixed / total


def attention_kernel(lengths_ref, q_ref, k_ref, v_ref, kn_ref, vn_ref, kf_ref, vf_ref, o_ref, bias_ref):
    first_row = lax.axis_index("ctx") * ROWS
    starts = row_starts(lengths_ref[...], first_row)
    bias_ref[...] = key_bias(starts, first_row, first_row - 2 * ROWS, 3 * ROWS)

    def chunk(i, carry):
        for h in range(2):
            at = pl.ds(pl.multiple_of(i * 2 * HEAD_DIM + h * HEAD_DIM, HEAD_DIM), HEAD_DIM)
            keys = jnp.concatenate([kf_ref[:, at], kn_ref[:, at], k_ref[:, at]], axis=0)
            values = jnp.concatenate([vf_ref[:, at], vn_ref[:, at], v_ref[:, at]], axis=0)
            o_ref[:, at] = attend_head(q_ref[:, at], keys, values, bias_ref[...]).astype(BF16)
        return carry

    lax.fori_loop(0, q_ref.shape[1] // HEAD_DIM // 2, chunk, 0)


def filter_rows(filters):
    tap = lax.broadcasted_iota(jnp.int32, (TAPS, 2 * TAPS), 0)
    column = lax.broadcasted_iota(jnp.int32, (TAPS, 2 * TAPS), 1)
    place = (column == TAPS - tap).astype(F32).astype(BF16)
    return jnp.dot(filters, place, preferred_element_type=F32)


def build_block(base, keeper, index, matrix_ref):
    for g in range(LANES // GROUP):
        spread = jnp.broadcast_to(base[g : g + 1], (ROWS, 2 * TAPS))
        band = pltpu.roll(spread, 0, 1, stride=1, stride_axis=0)
        matrix_ref[index, :, g * 2 * TAPS : (g + 1) * 2 * TAPS] = (band * keeper).astype(BF16)


def window_keeper(starts, first_row):
    position = (first_row - TAPS + lax.broadcasted_iota(jnp.int32, (ROWS, 2 * TAPS), 1)).astype(F32)
    return (position >= starts).astype(F32)


def conv_block(matrix, window):
    group = lax.broadcasted_iota(jnp.int32, window.shape, 1) // GROUP
    parts = [jnp.where(group == g, window, jnp.zeros_like(window)) for g in range(LANES // GROUP)]
    return jnp.dot(matrix, jnp.concatenate(parts, axis=0), preferred_element_type=F32)


def row_scale(ref):
    blocks = ref.shape[1] // LANES
    total = jnp.zeros((ROWS, LANES), F32)
    for b in range(blocks):
        piece = ref[:, b * LANES : (b + 1) * LANES].astype(F32)
        total = total + piece * piece
    mean = jnp.sum(total, axis=1, keepdims=True) * (1.0 / ref.shape[1])
    return lax.rsqrt(mean + 1e-06)


def conv_kernel(lengths_ref, halo_ref, att_ref, gain_ref, filters_ref, bypass_ref, o_ref, base_ref, matrix_ref):
    first_row = lax.axis_index("ctx") * ROWS
    starts = row_starts(lengths_ref[...], first_row)
    keeper = window_keeper(starts, first_row)
    base_ref[...] = filter_rows(filters_ref[...])
    blocks = att_ref.shape[1] // LANES

    def build(i, carry):
        build_block(base_ref[pl.ds(pl.multiple_of(i * 8, 8), 8), :], keeper, i, matrix_ref)
        return carry

    lax.fori_loop(0, blocks, build, 0)
    near_scale = row_scale(att_ref)
    far_scale = row_scale(halo_ref)

    def mix(i, carry):
        at = pl.ds(pl.multiple_of(i * LANES, LANES), LANES)
        gain = gain_ref[:, at]
        near = (att_ref[:, at].astype(F32) * near_scale * gain).astype(BF16)
        far = (halo_ref[:, at].astype(F32) * far_scale * gain).astype(BF16)
        summed = conv_block(matrix_ref[i], jnp.concatenate([far, near], axis=0))
        o_ref[:, at] = (summed + bypass_ref[:, at] * near.astype(F32)).astype(BF16)
        return carry

    lax.fori_loop(0, blocks, mix, 0)


def shards(queries, key_rows, value_rows, lengths, norm_gain, filters, bypass):
    width = queries.shape[1]
    vmem = pl.BlockSpec(memory_space=pltpu.VMEM)
    lengths = lengths.reshape(1, -1)
    near_keys, near_values = passed_along((key_rows, value_rows), "ctx", 1)
    far_keys, far_values = passed_along((key_rows, value_rows), "ctx", 2)
    attended = pl.pallas_call(
        attention_kernel,
        out_shape=jax.ShapeDtypeStruct((ROWS, width), BF16),
        in_specs=[vmem] * 8,
        out_specs=vmem,
        scratch_shapes=[pltpu.VMEM((ROWS, 3 * ROWS), F32)],
        name="attention",
    )(lengths, queries, key_rows, value_rows, near_keys, near_values, far_keys, far_values)
    halo = passed_along(attended, "ctx", 1)
    return pl.pallas_call(
        conv_kernel,
        out_shape=jax.ShapeDtypeStruct((ROWS, width), BF16),
        in_specs=[vmem] * 6,
        out_specs=vmem,
        scratch_shapes=[
            pltpu.VMEM((filters.shape[0], 2 * TAPS), F32),
            pltpu.VMEM((width // LANES, ROWS, LANES // GROUP * 2 * TAPS), BF16),
        ],
        compiler_params=pltpu.CompilerParams(vmem_limit_bytes=48 * 2**20),
        name="conv",
    )(lengths, halo, attended, norm_gain.reshape(1, -1), filters, bypass.reshape(1, -1))


def solution(mesh):
    rows = P(("dp", "ctx"), None)
    return jax.shard_map(
        shards, mesh=mesh, in_specs=(rows, rows, rows, P("dp"), P(), P(), P()), out_specs=rows, check_vma=False
    )
```

```python
import functools
import math

import jax
import jax.numpy as jnp
from jax import lax
from jax.experimental import pallas as pl
from jax.experimental.pallas import tpu as pltpu
from jax.sharding import PartitionSpec as P

HEAD_DIM = 128
ROWS = 128
TAPS = 128
GROUP = 16
LANES = 128
STATS = 16
CHUNK_HEADS = 2
WIDTH = CHUNK_HEADS * HEAD_DIM
AHEAD = 4
F32 = jnp.float32
BF16 = jnp.bfloat16
EXPONENT = math.log2(math.e) / math.sqrt(HEAD_DIM)
MASKED = -1e30
MESH = pl.DeviceIdType.MESH


def row_starts(lengths_row, first_row):
    docs = lengths_row.shape[1]
    upto = (
        lax.broadcasted_iota(jnp.int32, (docs, docs), 0) <= lax.broadcasted_iota(jnp.int32, (docs, docs), 1)
    ).astype(F32)
    sizes = jnp.broadcast_to(lengths_row.astype(F32), (8, docs))
    ends = jnp.dot(sizes.astype(BF16), upto.astype(BF16), preferred_element_type=F32)
    position = (first_row + lax.broadcasted_iota(jnp.int32, (ROWS, docs), 0)).astype(F32)
    passed = jnp.broadcast_to(ends[0:1], (ROWS, docs)) <= position
    return jnp.sum(jnp.where(passed, jnp.broadcast_to(sizes[0:1], (ROWS, docs)), 0.0), axis=1, keepdims=True)


def key_bias(starts, first_row, key_first, span):
    query_pos = (first_row + lax.broadcasted_iota(jnp.int32, (ROWS, span), 0)).astype(F32)
    key_pos = (key_first + lax.broadcasted_iota(jnp.int32, (ROWS, span), 1)).astype(F32)
    valid = (key_pos >= starts) & (key_pos <= query_pos)
    return jnp.where(valid, 0.0, MASKED)


def attend(query, keys, values, bias):
    scores = lax.dot_general(query, keys, (((1,), (1,)), ((), ())), preferred_element_type=F32) + bias
    top = jnp.max(scores, axis=1, keepdims=True)
    raised = jnp.exp2((scores - top) * EXPONENT)
    total = jnp.sum(raised, axis=1, keepdims=True)
    return jnp.dot(raised.astype(BF16), values, preferred_element_type=F32), total, top


def diagonal():
    return lax.broadcasted_iota(jnp.int32, (ROWS, ROWS), 0) == lax.broadcasted_iota(jnp.int32, (ROWS, ROWS), 1)


def pieces_of(column):
    row = jnp.sum(jnp.where(diagonal(), jnp.broadcast_to(column, (ROWS, ROWS)), 0.0), axis=0, keepdims=True)
    high = row.astype(BF16).astype(F32)
    middle = (row - high).astype(BF16).astype(F32)
    low = row - high - middle
    index = lax.broadcasted_iota(jnp.int32, (STATS, ROWS), 0)
    shape = (STATS, ROWS)
    rest = jnp.where(index == 2, jnp.broadcast_to(low, shape), 0.0)
    rest = jnp.where(index == 1, jnp.broadcast_to(middle, shape), rest)
    return jnp.where(index == 0, jnp.broadcast_to(high, shape), rest).astype(BF16)


def column_of(pieces):
    row = jnp.sum(pieces.astype(F32), axis=0, keepdims=True)
    return jnp.sum(jnp.where(diagonal(), jnp.broadcast_to(row, (ROWS, ROWS)), 0.0), axis=1, keepdims=True)


def filter_rows(filters):
    tap = lax.broadcasted_iota(jnp.int32, (TAPS, 2 * TAPS), 0)
    column = lax.broadcasted_iota(jnp.int32, (TAPS, 2 * TAPS), 1)
    place = (column == TAPS - tap).astype(F32).astype(BF16)
    return jnp.dot(filters, place, preferred_element_type=F32)


def build_block(base, keeper, index, matrix_ref):
    for g in range(LANES // GROUP):
        spread = jnp.broadcast_to(base[g : g + 1], (ROWS, 2 * TAPS))
        band = pltpu.roll(spread, 0, 1, stride=1, stride_axis=0)
        matrix_ref[index, :, g * 2 * TAPS : (g + 1) * 2 * TAPS] = (band * keeper).astype(BF16)


def window_keeper(starts, first_row):
    position = (first_row - TAPS + lax.broadcasted_iota(jnp.int32, (ROWS, 2 * TAPS), 1)).astype(F32)
    return (position >= starts).astype(F32)


def conv_block(matrix, window):
    group = lax.broadcasted_iota(jnp.int32, window.shape, 1) // GROUP
    parts = [jnp.where(group == g, window, jnp.zeros_like(window)) for g in range(LANES // GROUP)]
    return jnp.dot(matrix, jnp.concatenate(parts, axis=0), preferred_element_type=F32)


def scale_of(squares, width):
    return lax.rsqrt(jnp.sum(squares, axis=1, keepdims=True) * (1.0 / width) + 1e-06)


def device(place, row):
    return {"ctx": place, "dp": row}


def place_of(z, half, x, core):
    return ((z * 2 + half) * 4 + x) * 2 + core


def kernel(
    depth,
    chunks,
    lengths_ref,
    q_ref,
    k_ref,
    v_ref,
    gain_ref,
    filters_ref,
    bypass_ref,
    o_ref,
    att_ref,
    past_k,
    past_v,
    side_k,
    side_v,
    far_q,
    halo,
    sent_v,
    bias_ref,
    keep_ref,
    square_ref,
    base_ref,
    matrix_ref,
    r_past_k,
    r_past_v,
    r_side_k,
    r_side_v,
    r_far_q,
    r_halo,
    s_first,
    s_second,
    s_third,
    s_past_k,
    s_past_v,
    s_relay_k,
    s_relay_v,
    s_relay_h,
    s_relay_q,
):
    me, row = lax.axis_index("ctx"), lax.axis_index("dp")
    core, x, half, z = me % 2, (me // 2) % 4, (me // 8) % 2, me // 16
    other_row = (row + 2) % 4
    last, first = (x + 1) // 4, (3 - x) // 3
    mate = me + 1 - 2 * core
    left, right = core == 0, core == 1
    width = q_ref.shape[1]
    blocks = width // LANES
    per_chunk = WIDTH // LANES

    def columns(i):
        return pl.ds(pl.multiple_of(i * WIDTH, WIDTH), WIDTH)

    def onward(i, to_core):
        near = place_of(z, half, x + 1, to_core)
        relay = place_of(z, i % 2, 0, half)
        return device(near * (1 - last) + relay * last, row + last * (other_row - row)), i + last * (chunks + i // 2 - i)

    def backward(i):
        near = place_of(z, half, x - 1, 1)
        relay = place_of((z + depth - 1 + half) % depth, i % 2, 3, half)
        return device(near * (1 - first) + relay * first, row + first * (other_row - row)), i + first * (chunks + i // 2 - i)

    relay_right = device(place_of((z + core) % depth, 1 - core, 0, 1), other_row)
    relay_left = device(place_of((z + core) % depth, 1 - core, 0, 0), other_row)
    relay_back = device(place_of(z, 1 - core, 3, 1), other_row)

    def copy(source, target, send, receive, to):
        return pltpu.make_async_remote_copy(
            src_ref=source, dst_ref=target, send_sem=send, recv_sem=receive, device_id=to, device_id_type=MESH
        )

    mate_id = device(mate, row)

    def send_q(i):
        to, slot = backward(i)
        return copy(q_ref.at[:, columns(i)], far_q.at[slot], s_first.at[i], r_far_q.at[slot], to)

    def send_side_k(i):
        return copy(k_ref.at[:, columns(i)], side_k.at[i], s_second.at[i], r_side_k.at[i], mate_id)

    def send_side_v(i):
        return copy(v_ref.at[:, columns(i)], side_v.at[i], s_third.at[i], r_side_v.at[i], mate_id)

    def send_side_halo(i):
        return copy(att_ref.at[:, columns(i)], halo.at[i], s_past_k.at[i], r_halo.at[i], mate_id)

    def send_k(i):
        to, slot = onward(i, 1)
        return copy(k_ref.at[:, columns(i)], past_k.at[slot], s_first.at[i], r_past_k.at[slot], to)

    def send_v(i):
        to, slot = onward(i, 1)
        return copy(sent_v.at[i], past_v.at[slot], s_second.at[i], r_past_v.at[slot], to)

    def send_halo(i):
        to, slot = onward(i, 0)
        return copy(att_ref.at[:, columns(i)], halo.at[slot], s_third.at[i], r_halo.at[slot], to)

    def share_k(i):
        return copy(past_k.at[i], past_k.at[i], s_past_k.at[i], r_past_k.at[i], mate_id)

    def share_v(i):
        return copy(past_v.at[i], past_v.at[i], s_past_v.at[i], r_past_v.at[i], mate_id)

    def pass_k(i):
        return copy(past_k.at[chunks + i // 2], past_k.at[i], s_relay_k.at[i // 2], r_past_k.at[i], relay_right)

    def pass_v(i):
        return copy(past_v.at[chunks + i // 2], past_v.at[i], s_relay_v.at[i // 2], r_past_v.at[i], relay_right)

    def pass_halo(i):
        return copy(halo.at[chunks + i // 2], halo.at[i], s_relay_h.at[i // 2], r_halo.at[i], relay_left)

    def pass_q(i):
        return copy(far_q.at[chunks + i // 2], far_q.at[i], s_relay_q.at[i // 2], r_far_q.at[i], relay_back)

    def await_slot(buffer, receive, slot):
        copy(buffer.at[slot], buffer.at[slot], receive.at[slot], receive.at[slot], mate_id).wait_recv()

    barrier = pltpu.get_barrier_semaphore()

    def greet(place, at_row):
        pl.semaphore_signal(barrier, inc=1, device_id=device(place, at_row), device_id_type=MESH)

    greet(mate, row)
    sender = place_of((z + depth - 1 + half) % depth, 0, 0, 1 - half)

    @pl.when(x > 0)
    def _():
        greet(place_of(z, half, x - 1, 1), row)

    @pl.when(x == 0)
    def _():
        for part in range(2):
            greet(sender + 8 * part, other_row)
        greet(place_of(z, core, 3, 1), other_row)

    @pl.when(right & (x < 3))
    def _():
        greet(place_of(z, half, x + 1, 0), row)

    @pl.when(right & (x == 3))
    def _():
        for part in range(2):
            greet(place_of(z, part, 3, 1 - half), other_row)

    @pl.when(x == 3)
    def _():
        greet(place_of((z + 1 - core) % depth, core, 0, 0), other_row)

    pl.semaphore_wait(barrier, 1 + core * 2 + (1 - core) * (1 + first) + 2 * first + last)

    @pl.when(left)
    def _():
        def start(i, carry):
            send_q(i).start()
            send_side_k(i).start()
            send_side_v(i).start()
            return carry

        lax.fori_loop(0, chunks, start, 0)

    @pl.when(right)
    def _():
        def start(i, carry):
            send_k(i).start()
            return carry

        lax.fori_loop(0, chunks, start, 0)

    first_row = me * ROWS
    starts = row_starts(lengths_ref[...], first_row)
    next_first = (me + 1) * ROWS
    next_starts = row_starts(lengths_ref[...], next_first)
    keep_ref[...] = window_keeper(starts, first_row)
    base_ref[...] = filter_rows(filters_ref[...])
    square_ref[...] = jnp.zeros_like(square_ref)

    @pl.when(right)
    def _():
        bias_ref[:, : 3 * ROWS] = key_bias(starts, first_row, first_row - 2 * ROWS, 3 * ROWS)
        bias_ref[:, 3 * ROWS :] = key_bias(next_starts, next_first, next_first - 2 * ROWS, 2 * ROWS)

    short_before = (starts[0:1] >= (first_row - ROWS).astype(F32)).astype(F32)

    @pl.when(left)
    def _():
        bias_ref[:, :ROWS] = jnp.where(
            jnp.broadcast_to(short_before, (ROWS, ROWS)) > 0.5,
            key_bias(starts, first_row, first_row - ROWS, ROWS),
            MASKED,
        )
        bias_ref[:, ROWS : 2 * ROWS] = key_bias(starts, first_row, first_row, ROWS)

    next_short = (next_starts[0:1] >= (next_first - ROWS).astype(F32)).astype(F32)

    def keep_result(i, h, result):
        rounded = result.astype(BF16)
        wide = rounded.astype(F32)
        square_ref[...] += wide * wide
        att_ref[:, pl.ds(pl.multiple_of(i * WIDTH + h * HEAD_DIM, HEAD_DIM), HEAD_DIM)] = rounded

    def own_right(i):
        for h in range(CHUNK_HEADS):
            at = pl.ds(pl.multiple_of(i * WIDTH + h * HEAD_DIM, HEAD_DIM), HEAD_DIM)
            inner = slice(h * HEAD_DIM, (h + 1) * HEAD_DIM)
            keys = jnp.concatenate([past_k[i, :, inner], side_k[i, :, inner], k_ref[:, at]], axis=0)
            values = jnp.concatenate([past_v[i, :ROWS, inner], side_v[i, :, inner], v_ref[:, at]], axis=0)
            mixed, total, _ = attend(q_ref[:, at], keys, values, bias_ref[:, : 3 * ROWS])
            keep_result(i, h, mixed / total)

    def far_right(i):
        for h in range(CHUNK_HEADS):
            at = pl.ds(pl.multiple_of(i * WIDTH + h * HEAD_DIM, HEAD_DIM), HEAD_DIM)
            inner = slice(h * HEAD_DIM, (h + 1) * HEAD_DIM)
            keys = jnp.concatenate([side_k[i, :, inner], k_ref[:, at]], axis=0)
            values = jnp.concatenate([side_v[i, :, inner], v_ref[:, at]], axis=0)
            mixed, total, top = attend(far_q[i, :, inner], keys, values, bias_ref[:, 3 * ROWS :])
            level = top * EXPONENT + jnp.log2(total)
            level = jnp.where(jnp.broadcast_to(next_short, level.shape) > 0.5, MASKED, level)
            sent_v[i, :ROWS, inner] = jnp.where(
                jnp.broadcast_to(next_short, mixed.shape) > 0.5, v_ref[:, at].astype(F32), mixed / total
            ).astype(BF16)
            sent_v[i, ROWS:, inner] = pieces_of(level)

    def own_left(i):
        for h in range(CHUNK_HEADS):
            at = pl.ds(pl.multiple_of(i * WIDTH + h * HEAD_DIM, HEAD_DIM), HEAD_DIM)
            inner = slice(h * HEAD_DIM, (h + 1) * HEAD_DIM)
            keys = jnp.concatenate([past_k[i, :, inner], k_ref[:, at]], axis=0)
            values = jnp.concatenate([past_v[i, :ROWS, inner], v_ref[:, at]], axis=0)
            mixed, total, top = attend(q_ref[:, at], keys, values, bias_ref[:, : 2 * ROWS])
            far_level = column_of(past_v[i, ROWS:, inner])
            near_level = top * EXPONENT
            level = jnp.maximum(near_level, far_level)
            near_share, far_share = jnp.exp2(near_level - level), jnp.exp2(far_level - level)
            far_mixed = past_v[i, :ROWS, inner].astype(F32)
            keep_result(i, h, (near_share * mixed + far_share * far_mixed) / (near_share * total + far_share))

    def relays_q(i):
        return (x == 3) & (i < chunks) & (i % 2 == half)

    def relays_on(i):
        return (x == 0) & (i >= 0) & (i < chunks) & (i % 2 == half)

    def relay_q(i):
        @pl.when(relays_q(i))
        def _():
            await_slot(far_q, r_far_q, chunks + i // 2)
            pass_q(i).start()

    def relay_halo(i):
        @pl.when(relays_on(i))
        def _():
            await_slot(halo, r_halo, chunks + i // 2)
            pass_halo(i).start()

    relay_q(0)

    def step(i, carry):
        now = i - AHEAD
        relay_q(i + 1)

        @pl.when(relays_on(i - 1))
        def _():
            await_slot(past_k, r_past_k, chunks + (i - 1) // 2)
            pass_k(i - 1).start()

        @pl.when(relays_on(i - 2))
        def _():
            await_slot(past_v, r_past_v, chunks + (i - 2) // 2)
            pass_v(i - 2).start()

        relay_halo(now - 2)

        @pl.when(now >= 0)
        def _():
            await_slot(past_k, r_past_k, now)
            await_slot(past_v, r_past_v, now)

            @pl.when(right)
            def _():
                share_k(now).start()
                share_v(now).start()
                own_right(now)

            @pl.when(left)
            def _():
                own_left(now)

        @pl.when((i < chunks) & right)
        def _():
            await_slot(far_q, r_far_q, i)
            await_slot(side_k, r_side_k, i)
            await_slot(side_v, r_side_v, i)
            far_right(i)

        @pl.when(i < chunks)
        def _():
            for part in range(per_chunk):
                index = i * per_chunk + part
                build_block(base_ref[pl.ds(pl.multiple_of(index * 8, 8), 8), :], keep_ref[...], index, matrix_ref)

        @pl.when((i < chunks) & right)
        def _():
            send_v(i).start()

        @pl.when((now >= 0) & right)
        def _():
            send_halo(now).start()

        @pl.when((now >= 0) & left)
        def _():
            send_side_halo(now).start()

        return carry

    lax.fori_loop(0, chunks + AHEAD, step, 0)
    relay_halo(chunks - 2)
    relay_halo(chunks - 1)
    near_scale = scale_of(square_ref[...], width)

    def gather(i, total):
        await_slot(halo, r_halo, i)
        for part in range(per_chunk):
            piece = halo[i, :, part * LANES : (part + 1) * LANES].astype(F32)
            total = total + piece * piece
        return total

    far_scale = scale_of(lax.fori_loop(0, chunks, gather, jnp.zeros((ROWS, LANES), F32)), width)

    def mix(i, carry):
        for part in range(per_chunk):
            at = pl.ds(pl.multiple_of(i * WIDTH + part * LANES, LANES), LANES)
            gain = gain_ref[:, at]
            near = (att_ref[:, at].astype(F32) * near_scale * gain).astype(BF16)
            far = (halo[i, :, part * LANES : (part + 1) * LANES].astype(F32) * far_scale * gain).astype(BF16)
            summed = conv_block(matrix_ref[i * per_chunk + part], jnp.concatenate([far, near], axis=0))
            o_ref[:, at] = (summed + bypass_ref[:, at] * near.astype(F32)).astype(BF16)
        return carry

    lax.fori_loop(0, chunks, mix, 0)

    def finish(i, carry):
        @pl.when(left)
        def _():
            for sent in (send_q, send_side_k, send_side_v, send_side_halo):
                sent(i).wait_send()

        @pl.when(right)
        def _():
            for sent in (send_k, send_v, send_halo, share_k, share_v):
                sent(i).wait_send()

        @pl.when(relays_q(i))
        def _():
            pass_q(i).wait_send()

        @pl.when(relays_on(i))
        def _():
            for sent in (pass_k, pass_v, pass_halo):
                sent(i).wait_send()

        return carry

    lax.fori_loop(0, chunks, finish, 0)


def shards(mesh, queries, key_rows, value_rows, lengths, norm_gain, filters, bypass):
    width = queries.shape[1]
    chunks = width // WIDTH
    slots = chunks + chunks // 2
    vmem = pl.BlockSpec(memory_space=pltpu.VMEM)
    many = pltpu.SemaphoreType.DMA((slots,))
    some = pltpu.SemaphoreType.DMA((chunks,))
    few = pltpu.SemaphoreType.DMA((chunks // 2,))
    return pl.pallas_call(
        functools.partial(kernel, mesh.shape["ctx"] // 16, chunks),
        out_shape=jax.ShapeDtypeStruct((ROWS, width), BF16),
        in_specs=[vmem] * 7,
        out_specs=vmem,
        scratch_shapes=[
            pltpu.VMEM((ROWS, width), BF16),
            pltpu.VMEM((slots, ROWS, WIDTH), BF16),
            pltpu.VMEM((slots, ROWS + STATS, WIDTH), BF16),
            pltpu.VMEM((chunks, ROWS, WIDTH), BF16),
            pltpu.VMEM((chunks, ROWS, WIDTH), BF16),
            pltpu.VMEM((slots, ROWS, WIDTH), BF16),
            pltpu.VMEM((slots, ROWS, WIDTH), BF16),
            pltpu.VMEM((chunks, ROWS + STATS, WIDTH), BF16),
            pltpu.VMEM((ROWS, 5 * ROWS), F32),
            pltpu.VMEM((ROWS, 2 * TAPS), F32),
            pltpu.VMEM((ROWS, LANES), F32),
            pltpu.VMEM((filters.shape[0], 2 * TAPS), F32),
            pltpu.VMEM((width // LANES, ROWS, LANES // GROUP * 2 * TAPS), BF16),
            many,
            many,
            some,
            some,
            many,
            many,
            some,
            some,
            some,
            some,
            some,
            few,
            few,
            few,
            few,
        ],
        compiler_params=pltpu.CompilerParams(
            collective_id=0, has_side_effects=True, vmem_limit_bytes=56 * 2**20
        ),
        name="layer",
    )(
        lengths.reshape(1, -1),
        queries,
        key_rows,
        value_rows,
        norm_gain.reshape(1, -1),
        filters,
        bypass.reshape(1, -1),
    )


def solution(mesh):
    rows = P(("dp", "ctx"), None)
    return jax.shard_map(
        functools.partial(shards, mesh),
        mesh=mesh,
        in_specs=(rows, rows, rows, P("dp"), P(), P(), P()),
        out_specs=rows,
        check_vma=False,
    )
```

```python
import functools
import math

import jax
import jax.numpy as jnp
from jax import lax
from jax.experimental import pallas as pl
from jax.experimental.pallas import tpu as pltpu
from jax.sharding import PartitionSpec as P

HEAD_DIM = 128
ROWS = 128
TAPS = 128
GROUP = 16
LANES = 128
STATS = 16
CHUNK_HEADS = 2
WIDTH = CHUNK_HEADS * HEAD_DIM
F32 = jnp.float32
BF16 = jnp.bfloat16
EXPONENT = math.log2(math.e) / math.sqrt(HEAD_DIM)
MASKED = -1e30
OWN_LAG = 6
HALO_LAG = 10
MESH = pl.DeviceIdType.MESH


def row_starts(lengths_row, first_row):
    docs = lengths_row.shape[1]
    upto = (
        lax.broadcasted_iota(jnp.int32, (docs, docs), 0) <= lax.broadcasted_iota(jnp.int32, (docs, docs), 1)
    ).astype(F32)
    sizes = jnp.broadcast_to(lengths_row.astype(F32), (8, docs))
    ends = jnp.dot(sizes.astype(BF16), upto.astype(BF16), preferred_element_type=F32)
    position = (first_row + lax.broadcasted_iota(jnp.int32, (ROWS, docs), 0)).astype(F32)
    passed = jnp.broadcast_to(ends[0:1], (ROWS, docs)) <= position
    return jnp.sum(jnp.where(passed, jnp.broadcast_to(sizes[0:1], (ROWS, docs)), 0.0), axis=1, keepdims=True)


def key_bias(starts, first_row, key_first, span):
    query_pos = (first_row + lax.broadcasted_iota(jnp.int32, (ROWS, span), 0)).astype(F32)
    key_pos = (key_first + lax.broadcasted_iota(jnp.int32, (ROWS, span), 1)).astype(F32)
    valid = (key_pos >= starts) & (key_pos <= query_pos)
    return jnp.where(valid, 0.0, MASKED)


def attend(query, keys, values, bias):
    scores = lax.dot_general(query, keys, (((1,), (1,)), ((), ())), preferred_element_type=F32) + bias
    top = jnp.max(scores, axis=1, keepdims=True)
    raised = jnp.exp2((scores - top) * EXPONENT)
    rounded = raised.astype(BF16)
    summed = jnp.dot(rounded, jnp.concatenate([values, jnp.ones_like(values)], axis=1), preferred_element_type=F32)
    return summed[:, :HEAD_DIM], summed[:, HEAD_DIM:], top


def diagonal():
    return lax.broadcasted_iota(jnp.int32, (ROWS, ROWS), 0) == lax.broadcasted_iota(jnp.int32, (ROWS, ROWS), 1)


def pieces_of(column):
    row = jnp.sum(jnp.where(diagonal(), jnp.broadcast_to(column, (ROWS, ROWS)), 0.0), axis=0, keepdims=True)
    high = row.astype(BF16).astype(F32)
    middle = (row - high).astype(BF16).astype(F32)
    low = row - high - middle
    index = lax.broadcasted_iota(jnp.int32, (STATS, ROWS), 0)
    shape = (STATS, ROWS)
    rest = jnp.where(index == 2, jnp.broadcast_to(low, shape), 0.0)
    rest = jnp.where(index == 1, jnp.broadcast_to(middle, shape), rest)
    return jnp.where(index == 0, jnp.broadcast_to(high, shape), rest).astype(BF16)


def column_of(pieces):
    row = jnp.sum(pieces.astype(F32), axis=0, keepdims=True)
    return jnp.sum(jnp.where(diagonal(), jnp.broadcast_to(row, (ROWS, ROWS)), 0.0), axis=1, keepdims=True)


def filter_rows(filters):
    tap = lax.broadcasted_iota(jnp.int32, (TAPS, 2 * TAPS), 0)
    column = lax.broadcasted_iota(jnp.int32, (TAPS, 2 * TAPS), 1)
    place = (column == TAPS - tap).astype(F32).astype(BF16)
    return jnp.dot(filters, place, preferred_element_type=F32)


def build_block(base, keeper, index, matrix_ref):
    for g in range(LANES // GROUP):
        spread = jnp.broadcast_to(base[g : g + 1], (ROWS, 2 * TAPS))
        band = pltpu.roll(spread, 0, 1, stride=1, stride_axis=0)
        matrix_ref[index, :, g * 2 * TAPS : (g + 1) * 2 * TAPS] = (band * keeper).astype(BF16)


def window_keeper(starts, first_row):
    position = (first_row - TAPS + lax.broadcasted_iota(jnp.int32, (ROWS, 2 * TAPS), 1)).astype(F32)
    return (position >= starts).astype(F32)


def conv_block(matrix, window):
    group = lax.broadcasted_iota(jnp.int32, window.shape, 1) // GROUP
    parts = [jnp.where(group == g, window, jnp.zeros_like(window)) for g in range(LANES // GROUP)]
    return jnp.dot(matrix, jnp.concatenate(parts, axis=0), preferred_element_type=F32)


def scale_of(squares, width):
    return lax.rsqrt(jnp.sum(squares, axis=1, keepdims=True) * (1.0 / width) + 1e-06)


def device(place, row):
    return {"ctx": place, "dp": row}


def kernel(
    depth,
    chunks,
    lengths_ref,
    q_ref,
    k_ref,
    v_ref,
    gain_ref,
    filters_ref,
    bypass_ref,
    o_ref,
    att_ref,
    past_k,
    past_v,
    side_k,
    side_v,
    far_q,
    halo,
    sent_v,
    bias_ref,
    keep_ref,
    square_ref,
    base_ref,
    matrix_ref,
    r_past_k,
    r_past_v,
    r_side_k,
    r_side_v,
    r_far_q,
    r_halo,
    s_first,
    s_second,
    s_third,
    s_past_k,
    s_past_v,
    s_relay_k,
    s_relay_v,
    s_relay_h,
    s_relay_q,
):
    me, row = lax.axis_index("ctx"), lax.axis_index("dp")
    core, x = me % 2, (me // 2) % 4
    chip, chips = me // 2, depth * 8
    last, first = (x + 1) // 4, (3 - x) // 3
    mate = me + 1 - 2 * core
    next_chip, past_chip = (chip + 1) % chips, (chip + chips - 1) % chips
    left, right = core == 0, core == 1
    width = q_ref.shape[1]
    blocks = width // LANES
    per_chunk = WIDTH // LANES

    def columns(i):
        return pl.ds(pl.multiple_of(i * WIDTH, WIDTH), WIDTH)

    head, tail = chip == 0, chip == chips - 1
    turn = 1 + (2 * x) % 3
    row_last = chip - x + 3

    def onward(i, to_core):
        relayed = last * ((i % 4 + 2) // 3)
        place = 2 * next_chip + to_core
        relay = 2 * (chip - 3 + (2 * (i % 4) + 1) % 3)
        return device(place + relayed * (relay - place), row), i + relayed * (chunks + i // 4 - i)

    def backward(i):
        relayed = first * (i % 2)
        place = 2 * past_chip + 1
        return device(place + relayed * (2 * (chip + 3) - place), row), i + relayed * (chunks + i // 2 - i)

    def relay_target(to_core):
        return device(2 * ((row_last + 1) % chips) + to_core, row)

    relay_back = device(2 * ((chip + chips - 4) % chips) + 1, row)

    def copy(source, target, send, receive, to):
        return pltpu.make_async_remote_copy(
            src_ref=source, dst_ref=target, send_sem=send, recv_sem=receive, device_id=to, device_id_type=MESH
        )

    mate_id = device(mate, row)

    def send_q(i):
        to, slot = backward(i)
        return copy(q_ref.at[:, columns(i)], far_q.at[slot], s_first.at[i], r_far_q.at[slot], to)

    def send_side_k(i):
        return copy(k_ref.at[:, columns(i)], side_k.at[i], s_second.at[i], r_side_k.at[i], mate_id)

    def send_side_v(i):
        return copy(v_ref.at[:, columns(i)], side_v.at[i], s_third.at[i], r_side_v.at[i], mate_id)

    def send_side_halo(i):
        return copy(att_ref.at[:, columns(i)], halo.at[i], s_past_k.at[i], r_halo.at[i], mate_id)

    def send_k(i):
        to, slot = onward(i, 1)
        return copy(k_ref.at[:, columns(i)], past_k.at[slot], s_first.at[i], r_past_k.at[slot], to)

    def send_v(i):
        to, slot = onward(i, 1)
        return copy(sent_v.at[i], past_v.at[slot], s_second.at[i], r_past_v.at[slot], to)

    def send_halo(i):
        to, slot = onward(i, 0)
        return copy(att_ref.at[:, columns(i)], halo.at[slot], s_third.at[i], r_halo.at[slot], to)

    def share_k(i):
        return copy(past_k.at[i], past_k.at[i], s_past_k.at[i], r_past_k.at[i], mate_id)

    def share_v(i):
        return copy(past_v.at[i], past_v.at[i], s_past_v.at[i], r_past_v.at[i], mate_id)

    def pass_on(buffer, send, receive, i, to, share=4):
        return copy(buffer.at[chunks + i // share], buffer.at[i], send.at[i // share], receive.at[i], to)

    def pass_k(i):
        return pass_on(past_k, s_relay_k, r_past_k, i, relay_target(1))

    def pass_v(i):
        return pass_on(past_v, s_relay_v, r_past_v, i, relay_target(1))

    def pass_halo(i):
        return pass_on(halo, s_relay_h, r_halo, i, relay_target(0))

    def pass_q(i):
        return pass_on(far_q, s_relay_q, r_far_q, i, relay_back, 2)

    def await_slot(buffer, receive, slot):
        copy(buffer.at[slot], buffer.at[slot], receive.at[slot], receive.at[slot], mate_id).wait_recv()

    barrier = pltpu.get_barrier_semaphore()

    def greet(place):
        pl.semaphore_signal(barrier, inc=1, device_id=device(place, row), device_id_type=MESH)

    greet(mate)
    greet(2 * past_chip + 1)

    @pl.when(x == 0)
    def _():
        for part in range(3):
            greet(2 * ((chip + chips - 4 + part) % chips))

    @pl.when(right)
    def _():
        greet(2 * next_chip)

    @pl.when(right & (x == 3))
    def _():
        greet(2 * ((chip + 4) % chips))

    @pl.when(left & (x < 3))
    def _():
        greet(2 * row_last + 1)

    @pl.when(left & (x == 3))
    def _():
        greet(2 * (chip - 3))

    pl.semaphore_wait(barrier, core * (3 + 3 * last) + (1 - core) * (4 + first - last))

    @pl.when(left)
    def _():
        def start(i, carry):
            @pl.when(chip > 0)
            def _():
                send_q(i).start()

            send_side_k(i).start()
            send_side_v(i).start()
            return carry

        lax.fori_loop(0, chunks, start, 0)

    @pl.when(right & (chip < chips - 1))
    def _():
        def start(i, carry):
            send_k(i).start()
            return carry

        lax.fori_loop(0, chunks, start, 0)

    @pl.when(right & head)
    def _():
        def clear(i, carry):
            past_k[i] = jnp.zeros(past_k.shape[1:], BF16)
            past_v[i, :ROWS] = jnp.zeros((ROWS, WIDTH), BF16)
            past_v[i, ROWS:] = jnp.full((STATS, WIDTH), MASKED, BF16)
            return carry

        lax.fori_loop(0, chunks, clear, 0)

    @pl.when(left & head)
    def _():
        def clear(i, carry):
            halo[i] = jnp.zeros(halo.shape[1:], BF16)
            return carry

        lax.fori_loop(0, chunks, clear, 0)

    first_row = me * ROWS
    starts = row_starts(lengths_ref[...], first_row)
    next_first = (me + 1) * ROWS
    next_starts = row_starts(lengths_ref[...], next_first)
    keep_ref[...] = window_keeper(starts, first_row)
    base_ref[...] = filter_rows(filters_ref[...])
    square_ref[...] = jnp.zeros_like(square_ref)

    @pl.when(right)
    def _():
        bias_ref[:, : 3 * ROWS] = key_bias(starts, first_row, first_row - 2 * ROWS, 3 * ROWS)
        bias_ref[:, 3 * ROWS :] = key_bias(next_starts, next_first, next_first - 2 * ROWS, 2 * ROWS)

    short_before = (starts[0:1] >= (first_row - ROWS).astype(F32)).astype(F32)

    @pl.when(left)
    def _():
        bias_ref[:, :ROWS] = jnp.where(
            jnp.broadcast_to(short_before, (ROWS, ROWS)) > 0.5,
            key_bias(starts, first_row, first_row - ROWS, ROWS),
            MASKED,
        )
        bias_ref[:, ROWS : 2 * ROWS] = key_bias(starts, first_row, first_row, ROWS)

    next_short = (next_starts[0:1] >= (next_first - ROWS).astype(F32)).astype(F32)

    def keep_result(i, h, result):
        rounded = result.astype(BF16)
        wide = rounded.astype(F32)
        square_ref[...] += wide * wide
        att_ref[:, pl.ds(pl.multiple_of(i * WIDTH + h * HEAD_DIM, HEAD_DIM), HEAD_DIM)] = rounded

    def own_right(i):
        for h in range(CHUNK_HEADS):
            at = pl.ds(pl.multiple_of(i * WIDTH + h * HEAD_DIM, HEAD_DIM), HEAD_DIM)
            inner = slice(h * HEAD_DIM, (h + 1) * HEAD_DIM)
            keys = jnp.concatenate([past_k[i, :, inner], side_k[i, :, inner], k_ref[:, at]], axis=0)
            values = jnp.concatenate([past_v[i, :ROWS, inner], side_v[i, :, inner], v_ref[:, at]], axis=0)
            mixed, total, _ = attend(q_ref[:, at], keys, values, bias_ref[:, : 3 * ROWS])
            keep_result(i, h, mixed / total)

    def far_right(i):
        for h in range(CHUNK_HEADS):
            at = pl.ds(pl.multiple_of(i * WIDTH + h * HEAD_DIM, HEAD_DIM), HEAD_DIM)
            inner = slice(h * HEAD_DIM, (h + 1) * HEAD_DIM)
            keys = jnp.concatenate([side_k[i, :, inner], k_ref[:, at]], axis=0)
            values = jnp.concatenate([side_v[i, :, inner], v_ref[:, at]], axis=0)
            mixed, total, top = attend(far_q[i, :, inner], keys, values, bias_ref[:, 3 * ROWS :])
            level = top * EXPONENT + jnp.log2(total)
            level = jnp.where(jnp.broadcast_to(next_short, level.shape) > 0.5, MASKED, level)
            sent_v[i, :ROWS, inner] = jnp.where(
                jnp.broadcast_to(next_short, mixed.shape) > 0.5, v_ref[:, at].astype(F32), mixed / total
            ).astype(BF16)
            sent_v[i, ROWS:, inner] = pieces_of(level)

    def own_left(i):
        for h in range(CHUNK_HEADS):
            at = pl.ds(pl.multiple_of(i * WIDTH + h * HEAD_DIM, HEAD_DIM), HEAD_DIM)
            inner = slice(h * HEAD_DIM, (h + 1) * HEAD_DIM)
            keys = jnp.concatenate([past_k[i, :, inner], k_ref[:, at]], axis=0)
            values = jnp.concatenate([past_v[i, :ROWS, inner], v_ref[:, at]], axis=0)
            mixed, total, top = attend(q_ref[:, at], keys, values, bias_ref[:, : 2 * ROWS])
            far_level = column_of(past_v[i, ROWS:, inner])
            near_level = top * EXPONENT
            level = jnp.maximum(near_level, far_level)
            near_share, far_share = jnp.exp2(near_level - level), jnp.exp2(far_level - level)
            far_mixed = past_v[i, :ROWS, inner].astype(F32)
            keep_result(i, h, (near_share * mixed + far_share * far_mixed) / (near_share * total + far_share))

    def relays_q(i):
        return left & (x == 3) & (chip > 3) & (i % 2 == 1)

    def relays_on(i):
        return left & (x < 3) & (row_last < chips - 1) & (i % 4 == turn)

    def build(i):
        for part in range(per_chunk):
            index = i * per_chunk + part
            build_block(base_ref[pl.ds(pl.multiple_of(index * 8, 8), 8), :], keep_ref[...], index, matrix_ref)

    @pl.when(right)
    def _():
        @pl.when(chip < chips - 1)
        def _():
            def early(i, carry):
                await_slot(far_q, r_far_q, i)
                await_slot(side_k, r_side_k, i)
                await_slot(side_v, r_side_v, i)
                far_right(i)
                send_v(i).start()
                return carry

            lax.fori_loop(0, chunks, early, 0)

        @pl.when(tail)
        def _():
            def early(i, carry):
                await_slot(side_k, r_side_k, i)
                await_slot(side_v, r_side_v, i)
                return carry

            lax.fori_loop(0, chunks, early, 0)

        def late(i, carry):
            @pl.when(chip > 0)
            def _():
                await_slot(past_k, r_past_k, i)
                await_slot(past_v, r_past_v, i)

            share_k(i).start()
            share_v(i).start()
            own_right(i)

            @pl.when(chip < chips - 1)
            def _():
                send_halo(i).start()

            return carry

        lax.fori_loop(0, chunks, late, 0)

        def rest(i, carry):
            build(i)
            return carry

        lax.fori_loop(0, chunks, rest, 0)

    @pl.when(left)
    def _():
        def early(i, carry):
            @pl.when(relays_q(i))
            def _():
                await_slot(far_q, r_far_q, chunks + i // 2)
                pass_q(i).start()

            @pl.when(relays_on(i))
            def _():
                await_slot(past_k, r_past_k, chunks + i // 4)
                pass_k(i).start()

            build(i)
            return carry

        lax.fori_loop(0, chunks, early, 0)

        def late(step, carry):
            @pl.when((step < chunks) & relays_on(step))
            def _():
                await_slot(past_v, r_past_v, chunks + step // 4)
                pass_v(step).start()

            now = step - OWN_LAG

            @pl.when((now >= 0) & (now < chunks))
            def _():
                await_slot(past_k, r_past_k, now)
                await_slot(past_v, r_past_v, now)
                own_left(now)
                send_side_halo(now).start()

            past = step - HALO_LAG

            @pl.when((past >= 0) & relays_on(past))
            def _():
                await_slot(halo, r_halo, chunks + past // 4)
                pass_halo(past).start()

            return carry

        lax.fori_loop(0, chunks + HALO_LAG, late, 0)

    near_scale = scale_of(square_ref[...], width)

    def gather(i, total):
        @pl.when(right | (chip > 0))
        def _():
            await_slot(halo, r_halo, i)

        for part in range(per_chunk):
            piece = halo[i, :, part * LANES : (part + 1) * LANES].astype(F32)
            total = total + piece * piece
        return total

    far_scale = scale_of(lax.fori_loop(0, chunks, gather, jnp.zeros((ROWS, LANES), F32)), width)

    def mix(i, carry):
        for part in range(per_chunk):
            at = pl.ds(pl.multiple_of(i * WIDTH + part * LANES, LANES), LANES)
            gain = gain_ref[:, at]
            near = (att_ref[:, at].astype(F32) * near_scale * gain).astype(BF16)
            far = (halo[i, :, part * LANES : (part + 1) * LANES].astype(F32) * far_scale * gain).astype(BF16)
            summed = conv_block(matrix_ref[i * per_chunk + part], jnp.concatenate([far, near], axis=0))
            o_ref[:, at] = (summed + bypass_ref[:, at] * near.astype(F32)).astype(BF16)
        return carry

    lax.fori_loop(0, chunks, mix, 0)

    def finish(i, carry):
        @pl.when(left)
        def _():
            for sent in (send_side_k, send_side_v, send_side_halo):
                sent(i).wait_send()

        @pl.when(left & (chip > 0))
        def _():
            send_q(i).wait_send()

        @pl.when(right)
        def _():
            for sent in (share_k, share_v):
                sent(i).wait_send()

        @pl.when(right & (chip < chips - 1))
        def _():
            for sent in (send_k, send_v, send_halo):
                sent(i).wait_send()

        @pl.when(relays_q(i))
        def _():
            pass_q(i).wait_send()

        @pl.when(relays_on(i))
        def _():
            for sent in (pass_k, pass_v, pass_halo):
                sent(i).wait_send()

        return carry

    lax.fori_loop(0, chunks, finish, 0)


def shards(mesh, queries, key_rows, value_rows, lengths, norm_gain, filters, bypass):
    width = queries.shape[1]
    chunks = width // WIDTH
    slots = chunks + chunks // 2
    vmem = pl.BlockSpec(memory_space=pltpu.VMEM)
    many = pltpu.SemaphoreType.DMA((slots,))
    some = pltpu.SemaphoreType.DMA((chunks,))
    few = pltpu.SemaphoreType.DMA((chunks // 2,))
    return pl.pallas_call(
        functools.partial(kernel, mesh.shape["ctx"] // 16, chunks),
        out_shape=jax.ShapeDtypeStruct((ROWS, width), BF16),
        in_specs=[vmem] * 7,
        out_specs=vmem,
        scratch_shapes=[
            pltpu.VMEM((ROWS, width), BF16),
            pltpu.VMEM((slots, ROWS, WIDTH), BF16),
            pltpu.VMEM((slots, ROWS + STATS, WIDTH), BF16),
            pltpu.VMEM((chunks, ROWS, WIDTH), BF16),
            pltpu.VMEM((chunks, ROWS, WIDTH), BF16),
            pltpu.VMEM((slots, ROWS, WIDTH), BF16),
            pltpu.VMEM((slots, ROWS, WIDTH), BF16),
            pltpu.VMEM((chunks, ROWS + STATS, WIDTH), BF16),
            pltpu.VMEM((ROWS, 5 * ROWS), F32),
            pltpu.VMEM((ROWS, 2 * TAPS), F32),
            pltpu.VMEM((ROWS, LANES), F32),
            pltpu.VMEM((filters.shape[0], 2 * TAPS), F32),
            pltpu.VMEM((width // LANES, ROWS, LANES // GROUP * 2 * TAPS), BF16),
            many,
            many,
            some,
            some,
            many,
            many,
            some,
            some,
            some,
            some,
            some,
            few,
            few,
            few,
            few,
        ],
        compiler_params=pltpu.CompilerParams(
            collective_id=0, has_side_effects=True, vmem_limit_bytes=56 * 2**20
        ),
        name="layer",
    )(
        lengths.reshape(1, -1),
        queries,
        key_rows,
        value_rows,
        norm_gain.reshape(1, -1),
        filters,
        bypass.reshape(1, -1),
    )


def solution(mesh):
    rows = P(("dp", "ctx"), None)
    return jax.shard_map(
        functools.partial(shards, mesh),
        mesh=mesh,
        in_specs=(rows, rows, rows, P("dp"), P(), P(), P()),
        out_specs=rows,
        check_vma=False,
    )
```

```python
import functools
import math

import jax
import jax.numpy as jnp
from jax import lax
from jax.experimental import pallas as pl
from jax.experimental.pallas import tpu as pltpu
from jax.sharding import PartitionSpec as P

HEAD_DIM = 128
ROWS = 128
TAPS = 128
GROUP = 16
LANES = 128
STATS = 16
CHUNK_HEADS = 2
WIDTH = CHUNK_HEADS * HEAD_DIM
F32 = jnp.float32
BF16 = jnp.bfloat16
EXPONENT = math.log2(math.e) / math.sqrt(HEAD_DIM)
MASKED = -1e30
OWN_LAG = 6
HALO_LAG = 10
MESH = pl.DeviceIdType.MESH


def row_starts(lengths_row, first_row):
    docs = lengths_row.shape[1]
    upto = (
        lax.broadcasted_iota(jnp.int32, (docs, docs), 0) <= lax.broadcasted_iota(jnp.int32, (docs, docs), 1)
    ).astype(F32)
    sizes = jnp.broadcast_to(lengths_row.astype(F32), (8, docs))
    ends = jnp.dot(sizes.astype(BF16), upto.astype(BF16), preferred_element_type=F32)
    position = (first_row + lax.broadcasted_iota(jnp.int32, (ROWS, docs), 0)).astype(F32)
    passed = jnp.broadcast_to(ends[0:1], (ROWS, docs)) <= position
    return jnp.sum(jnp.where(passed, jnp.broadcast_to(sizes[0:1], (ROWS, docs)), 0.0), axis=1, keepdims=True)


def key_bias(starts, first_row, key_first, span):
    query_pos = (first_row + lax.broadcasted_iota(jnp.int32, (ROWS, span), 0)).astype(F32)
    key_pos = (key_first + lax.broadcasted_iota(jnp.int32, (ROWS, span), 1)).astype(F32)
    valid = (key_pos >= starts) & (key_pos <= query_pos)
    return jnp.where(valid, 0.0, MASKED)


def attend(query, keys, values, bias):
    scores = lax.dot_general(query, keys, (((1,), (1,)), ((), ())), preferred_element_type=F32) + bias
    top = jnp.max(scores, axis=1, keepdims=True)
    raised = jnp.exp2((scores - top) * EXPONENT)
    rounded = raised.astype(BF16)
    summed = jnp.dot(rounded, jnp.concatenate([values, jnp.ones_like(values)], axis=1), preferred_element_type=F32)
    return summed[:, :HEAD_DIM], summed[:, HEAD_DIM:], top


def diagonal():
    return lax.broadcasted_iota(jnp.int32, (ROWS, ROWS), 0) == lax.broadcasted_iota(jnp.int32, (ROWS, ROWS), 1)


def pieces_of(column):
    row = jnp.sum(jnp.where(diagonal(), jnp.broadcast_to(column, (ROWS, ROWS)), 0.0), axis=0, keepdims=True)
    high = row.astype(BF16).astype(F32)
    middle = (row - high).astype(BF16).astype(F32)
    low = row - high - middle
    index = lax.broadcasted_iota(jnp.int32, (STATS, ROWS), 0)
    shape = (STATS, ROWS)
    rest = jnp.where(index == 2, jnp.broadcast_to(low, shape), 0.0)
    rest = jnp.where(index == 1, jnp.broadcast_to(middle, shape), rest)
    return jnp.where(index == 0, jnp.broadcast_to(high, shape), rest).astype(BF16)


def column_of(pieces):
    row = jnp.sum(pieces.astype(F32), axis=0, keepdims=True)
    return jnp.sum(jnp.where(diagonal(), jnp.broadcast_to(row, (ROWS, ROWS)), 0.0), axis=1, keepdims=True)


def filter_rows(filters):
    tap = lax.broadcasted_iota(jnp.int32, (TAPS, 2 * TAPS), 0)
    column = lax.broadcasted_iota(jnp.int32, (TAPS, 2 * TAPS), 1)
    place = (column == TAPS - tap).astype(F32).astype(BF16)
    return jnp.dot(filters, place, preferred_element_type=F32)


def build_block(base, keeper, index, matrix_ref):
    for g in range(LANES // GROUP):
        spread = jnp.broadcast_to(base[g : g + 1], (ROWS, 2 * TAPS))
        band = pltpu.roll(spread, 0, 1, stride=1, stride_axis=0)
        matrix_ref[index, :, g * 2 * TAPS : (g + 1) * 2 * TAPS] = (band * keeper).astype(BF16)


def window_keeper(starts, first_row):
    position = (first_row - TAPS + lax.broadcasted_iota(jnp.int32, (ROWS, 2 * TAPS), 1)).astype(F32)
    return (position >= starts).astype(F32)


def conv_block(matrix, window):
    group = lax.broadcasted_iota(jnp.int32, window.shape, 1) // GROUP
    parts = [jnp.where(group == g, window, jnp.zeros_like(window)) for g in range(LANES // GROUP)]
    return jnp.dot(matrix, jnp.concatenate(parts, axis=0), preferred_element_type=F32)


def scale_of(squares, width):
    return lax.rsqrt(jnp.sum(squares, axis=1, keepdims=True) * (1.0 / width) + 1e-06)


def device(place, row):
    return {"ctx": place, "dp": row}


def kernel(
    depth,
    chunks,
    lengths_ref,
    q_ref,
    k_ref,
    v_ref,
    gain_ref,
    filters_ref,
    bypass_ref,
    o_ref,
    att_ref,
    past_k,
    past_v,
    side_k,
    side_v,
    far_q,
    halo,
    sent_v,
    bias_ref,
    keep_ref,
    square_ref,
    base_ref,
    matrix_ref,
    r_past_k,
    r_past_v,
    r_side_k,
    r_side_v,
    r_far_q,
    r_halo,
    s_first,
    s_second,
    s_third,
    s_past_k,
    s_past_v,
    s_relay_k,
    s_relay_v,
    s_relay_h,
    s_relay_q,
):
    me, row = lax.axis_index("ctx"), lax.axis_index("dp")
    core, x = me % 2, (me // 2) % 4
    chip, chips = me // 2, depth * 8
    last, first = (x + 1) // 4, (3 - x) // 3
    mate = me + 1 - 2 * core
    next_chip, past_chip = (chip + 1) % chips, (chip + chips - 1) % chips
    left, right = core == 0, core == 1
    width = q_ref.shape[1]
    blocks = width // LANES
    per_chunk = WIDTH // LANES

    def columns(i):
        return pl.ds(pl.multiple_of(i * WIDTH, WIDTH), WIDTH)

    head, tail = chip == 0, chip == chips - 1
    turn = 1 + (2 * x) % 3
    row_last = chip - x + 3

    def onward(i, to_core):
        relayed = last * ((i % 4 + 2) // 3)
        place = 2 * next_chip + to_core
        relay = 2 * (chip - 3 + (2 * (i % 4) + 1) % 3)
        return device(place + relayed * (relay - place), row), i + relayed * (chunks + i // 4 - i)

    def backward(i):
        relayed = first * ((i % 4 + 2) // 3)
        place = 2 * past_chip + 1
        relay = 2 * (chip + 1 + (2 * (i % 4)) % 3)
        return device(place + relayed * (relay - place), row), i + relayed * (chunks + i // 4 - i)

    def relay_target(to_core):
        return device(2 * ((row_last + 1) % chips) + to_core, row)

    relay_back = device(2 * ((chip - x + chips - 1) % chips) + 1, row)

    def copy(source, target, send, receive, to):
        return pltpu.make_async_remote_copy(
            src_ref=source, dst_ref=target, send_sem=send, recv_sem=receive, device_id=to, device_id_type=MESH
        )

    mate_id = device(mate, row)

    def send_q(i):
        to, slot = backward(i)
        return copy(q_ref.at[:, columns(i)], far_q.at[slot], s_first.at[i], r_far_q.at[slot], to)

    def send_side_k(i):
        return copy(k_ref.at[:, columns(i)], side_k.at[i], s_second.at[i], r_side_k.at[i], mate_id)

    def send_side_v(i):
        return copy(v_ref.at[:, columns(i)], side_v.at[i], s_third.at[i], r_side_v.at[i], mate_id)

    def send_side_halo(i):
        return copy(att_ref.at[:, columns(i)], halo.at[i], s_past_k.at[i], r_halo.at[i], mate_id)

    def send_k(i):
        to, slot = onward(i, 1)
        return copy(k_ref.at[:, columns(i)], past_k.at[slot], s_first.at[i], r_past_k.at[slot], to)

    def send_v(i):
        to, slot = onward(i, 1)
        return copy(sent_v.at[i], past_v.at[slot], s_second.at[i], r_past_v.at[slot], to)

    def send_halo(i):
        to, slot = onward(i, 0)
        return copy(att_ref.at[:, columns(i)], halo.at[slot], s_third.at[i], r_halo.at[slot], to)

    def share_k(i):
        return copy(past_k.at[i], past_k.at[i], s_past_k.at[i], r_past_k.at[i], mate_id)

    def share_v(i):
        return copy(past_v.at[i], past_v.at[i], s_past_v.at[i], r_past_v.at[i], mate_id)

    def pass_on(buffer, send, receive, i, to, share=4):
        return copy(buffer.at[chunks + i // share], buffer.at[i], send.at[i // share], receive.at[i], to)

    def pass_k(i):
        return pass_on(past_k, s_relay_k, r_past_k, i, relay_target(1))

    def pass_v(i):
        return pass_on(past_v, s_relay_v, r_past_v, i, relay_target(1))

    def pass_halo(i):
        return pass_on(halo, s_relay_h, r_halo, i, relay_target(0))

    def pass_q(i):
        return pass_on(far_q, s_relay_q, r_far_q, i, relay_back)

    def await_slot(buffer, receive, slot):
        copy(buffer.at[slot], buffer.at[slot], receive.at[slot], receive.at[slot], mate_id).wait_recv()

    barrier = pltpu.get_barrier_semaphore()

    def greet(place):
        pl.semaphore_signal(barrier, inc=1, device_id=device(place, row), device_id_type=MESH)

    greet(mate)
    greet(2 * past_chip + 1)

    @pl.when(x == 0)
    def _():
        for part in range(3):
            greet(2 * ((chip + chips - 4 + part) % chips))

    @pl.when(right)
    def _():
        greet(2 * next_chip)

    @pl.when(right & (x == 3))
    def _():
        for part in range(3):
            greet(2 * ((chip + 2 + part) % chips))

    @pl.when(left & (x < 3))
    def _():
        greet(2 * row_last + 1)

    @pl.when(left & (x > 0))
    def _():
        greet(2 * (chip - x))

    pl.semaphore_wait(barrier, core * (3 + 3 * last) + (1 - core) * (5 + 2 * first - 2 * last))

    @pl.when(left)
    def _():
        def start(i, carry):
            @pl.when(chip > 0)
            def _():
                send_q(i).start()

            send_side_k(i).start()
            send_side_v(i).start()
            return carry

        lax.fori_loop(0, chunks, start, 0)

    @pl.when(right & (chip < chips - 1))
    def _():
        def start(i, carry):
            send_k(i).start()
            return carry

        lax.fori_loop(0, chunks, start, 0)

    @pl.when(right & head)
    def _():
        def clear(i, carry):
            past_k[i] = jnp.zeros(past_k.shape[1:], BF16)
            past_v[i, :ROWS] = jnp.zeros((ROWS, WIDTH), BF16)
            past_v[i, ROWS:] = jnp.full((STATS, WIDTH), MASKED, BF16)
            return carry

        lax.fori_loop(0, chunks, clear, 0)

    @pl.when(left & head)
    def _():
        def clear(i, carry):
            halo[i] = jnp.zeros(halo.shape[1:], BF16)
            return carry

        lax.fori_loop(0, chunks, clear, 0)

    first_row = me * ROWS
    starts = row_starts(lengths_ref[...], first_row)
    next_first = (me + 1) * ROWS
    next_starts = row_starts(lengths_ref[...], next_first)
    keep_ref[...] = window_keeper(starts, first_row)
    base_ref[...] = filter_rows(filters_ref[...])
    square_ref[...] = jnp.zeros_like(square_ref)

    @pl.when(right)
    def _():
        bias_ref[:, : 3 * ROWS] = key_bias(starts, first_row, first_row - 2 * ROWS, 3 * ROWS)
        bias_ref[:, 3 * ROWS :] = key_bias(next_starts, next_first, next_first - 2 * ROWS, 2 * ROWS)

    short_before = (starts[0:1] >= (first_row - ROWS).astype(F32)).astype(F32)

    @pl.when(left)
    def _():
        bias_ref[:, :ROWS] = jnp.where(
            jnp.broadcast_to(short_before, (ROWS, ROWS)) > 0.5,
            key_bias(starts, first_row, first_row - ROWS, ROWS),
            MASKED,
        )
        bias_ref[:, ROWS : 2 * ROWS] = key_bias(starts, first_row, first_row, ROWS)

    next_short = (next_starts[0:1] >= (next_first - ROWS).astype(F32)).astype(F32)

    def keep_result(i, h, result):
        rounded = result.astype(BF16)
        wide = rounded.astype(F32)
        square_ref[...] += wide * wide
        att_ref[:, pl.ds(pl.multiple_of(i * WIDTH + h * HEAD_DIM, HEAD_DIM), HEAD_DIM)] = rounded

    def own_right(i):
        for h in range(CHUNK_HEADS):
            at = pl.ds(pl.multiple_of(i * WIDTH + h * HEAD_DIM, HEAD_DIM), HEAD_DIM)
            inner = slice(h * HEAD_DIM, (h + 1) * HEAD_DIM)
            keys = jnp.concatenate([past_k[i, :, inner], side_k[i, :, inner], k_ref[:, at]], axis=0)
            values = jnp.concatenate([past_v[i, :ROWS, inner], side_v[i, :, inner], v_ref[:, at]], axis=0)
            mixed, total, _ = attend(q_ref[:, at], keys, values, bias_ref[:, : 3 * ROWS])
            keep_result(i, h, mixed / total)

    def far_right(i):
        for h in range(CHUNK_HEADS):
            at = pl.ds(pl.multiple_of(i * WIDTH + h * HEAD_DIM, HEAD_DIM), HEAD_DIM)
            inner = slice(h * HEAD_DIM, (h + 1) * HEAD_DIM)
            keys = jnp.concatenate([side_k[i, :, inner], k_ref[:, at]], axis=0)
            values = jnp.concatenate([side_v[i, :, inner], v_ref[:, at]], axis=0)
            mixed, total, top = attend(far_q[i, :, inner], keys, values, bias_ref[:, 3 * ROWS :])
            level = top * EXPONENT + jnp.log2(total)
            level = jnp.where(jnp.broadcast_to(next_short, level.shape) > 0.5, MASKED, level)
            sent_v[i, :ROWS, inner] = jnp.where(
                jnp.broadcast_to(next_short, mixed.shape) > 0.5, v_ref[:, at].astype(F32), mixed / total
            ).astype(BF16)
            sent_v[i, ROWS:, inner] = pieces_of(level)

    def own_left(i):
        for h in range(CHUNK_HEADS):
            at = pl.ds(pl.multiple_of(i * WIDTH + h * HEAD_DIM, HEAD_DIM), HEAD_DIM)
            inner = slice(h * HEAD_DIM, (h + 1) * HEAD_DIM)
            keys = jnp.concatenate([past_k[i, :, inner], k_ref[:, at]], axis=0)
            values = jnp.concatenate([past_v[i, :ROWS, inner], v_ref[:, at]], axis=0)
            mixed, total, top = attend(q_ref[:, at], keys, values, bias_ref[:, : 2 * ROWS])
            far_level = column_of(past_v[i, ROWS:, inner])
            near_level = top * EXPONENT
            level = jnp.maximum(near_level, far_level)
            near_share, far_share = jnp.exp2(near_level - level), jnp.exp2(far_level - level)
            far_mixed = past_v[i, :ROWS, inner].astype(F32)
            keep_result(i, h, (near_share * mixed + far_share * far_mixed) / (near_share * total + far_share))

    def relays_q(i):
        return left & (x > 0) & (chip > x) & (i % 4 == 4 - x)

    def relays_on(i):
        return left & (x < 3) & (row_last < chips - 1) & (i % 4 == turn)

    def build(i):
        for part in range(per_chunk):
            index = i * per_chunk + part
            build_block(base_ref[pl.ds(pl.multiple_of(index * 8, 8), 8), :], keep_ref[...], index, matrix_ref)

    @pl.when(right)
    def _():
        @pl.when(chip < chips - 1)
        def _():
            def early(i, carry):
                await_slot(far_q, r_far_q, i)
                await_slot(side_k, r_side_k, i)
                await_slot(side_v, r_side_v, i)
                far_right(i)
                send_v(i).start()
                return carry

            lax.fori_loop(0, chunks, early, 0)

        @pl.when(tail)
        def _():
            def early(i, carry):
                await_slot(side_k, r_side_k, i)
                await_slot(side_v, r_side_v, i)
                return carry

            lax.fori_loop(0, chunks, early, 0)

        def late(i, carry):
            @pl.when(chip > 0)
            def _():
                await_slot(past_k, r_past_k, i)
                await_slot(past_v, r_past_v, i)

            share_k(i).start()
            share_v(i).start()
            own_right(i)

            @pl.when(chip < chips - 1)
            def _():
                send_halo(i).start()

            return carry

        lax.fori_loop(0, chunks, late, 0)

        def rest(i, carry):
            build(i)
            return carry

        lax.fori_loop(0, chunks, rest, 0)

    @pl.when(left)
    def _():
        def early(i, carry):
            @pl.when(relays_q(i))
            def _():
                await_slot(far_q, r_far_q, chunks + i // 4)
                pass_q(i).start()

            @pl.when(relays_on(i))
            def _():
                await_slot(past_k, r_past_k, chunks + i // 4)
                pass_k(i).start()

            build(i)
            return carry

        lax.fori_loop(0, chunks, early, 0)

        def late(step, carry):
            @pl.when((step < chunks) & relays_on(step))
            def _():
                await_slot(past_v, r_past_v, chunks + step // 4)
                pass_v(step).start()

            now = step - OWN_LAG

            @pl.when((now >= 0) & (now < chunks))
            def _():
                await_slot(past_k, r_past_k, now)
                await_slot(past_v, r_past_v, now)
                own_left(now)
                send_side_halo(now).start()

            past = step - HALO_LAG

            @pl.when((past >= 0) & relays_on(past))
            def _():
                await_slot(halo, r_halo, chunks + past // 4)
                pass_halo(past).start()

            return carry

        lax.fori_loop(0, chunks + HALO_LAG, late, 0)

    near_scale = scale_of(square_ref[...], width)

    def gather(i, total):
        @pl.when(right | (chip > 0))
        def _():
            await_slot(halo, r_halo, i)

        for part in range(per_chunk):
            piece = halo[i, :, part * LANES : (part + 1) * LANES].astype(F32)
            total = total + piece * piece
        return total

    far_scale = scale_of(lax.fori_loop(0, chunks, gather, jnp.zeros((ROWS, LANES), F32)), width)

    def mix(i, carry):
        for part in range(per_chunk):
            at = pl.ds(pl.multiple_of(i * WIDTH + part * LANES, LANES), LANES)
            gain = gain_ref[:, at]
            near = (att_ref[:, at].astype(F32) * near_scale * gain).astype(BF16)
            far = (halo[i, :, part * LANES : (part + 1) * LANES].astype(F32) * far_scale * gain).astype(BF16)
            summed = conv_block(matrix_ref[i * per_chunk + part], jnp.concatenate([far, near], axis=0))
            o_ref[:, at] = (summed + bypass_ref[:, at] * near.astype(F32)).astype(BF16)
        return carry

    lax.fori_loop(0, chunks, mix, 0)

    def finish(i, carry):
        @pl.when(left)
        def _():
            for sent in (send_side_k, send_side_v, send_side_halo):
                sent(i).wait_send()

        @pl.when(left & (chip > 0))
        def _():
            send_q(i).wait_send()

        @pl.when(right)
        def _():
            for sent in (share_k, share_v):
                sent(i).wait_send()

        @pl.when(right & (chip < chips - 1))
        def _():
            for sent in (send_k, send_v, send_halo):
                sent(i).wait_send()

        @pl.when(relays_q(i))
        def _():
            pass_q(i).wait_send()

        @pl.when(relays_on(i))
        def _():
            for sent in (pass_k, pass_v, pass_halo):
                sent(i).wait_send()

        return carry

    lax.fori_loop(0, chunks, finish, 0)


def shards(mesh, queries, key_rows, value_rows, lengths, norm_gain, filters, bypass):
    width = queries.shape[1]
    chunks = width // WIDTH
    slots = chunks + chunks // 2
    vmem = pl.BlockSpec(memory_space=pltpu.VMEM)
    many = pltpu.SemaphoreType.DMA((slots,))
    some = pltpu.SemaphoreType.DMA((chunks,))
    few = pltpu.SemaphoreType.DMA((chunks // 2,))
    return pl.pallas_call(
        functools.partial(kernel, mesh.shape["ctx"] // 16, chunks),
        out_shape=jax.ShapeDtypeStruct((ROWS, width), BF16),
        in_specs=[vmem] * 7,
        out_specs=vmem,
        scratch_shapes=[
            pltpu.VMEM((ROWS, width), BF16),
            pltpu.VMEM((slots, ROWS, WIDTH), BF16),
            pltpu.VMEM((slots, ROWS + STATS, WIDTH), BF16),
            pltpu.VMEM((chunks, ROWS, WIDTH), BF16),
            pltpu.VMEM((chunks, ROWS, WIDTH), BF16),
            pltpu.VMEM((slots, ROWS, WIDTH), BF16),
            pltpu.VMEM((slots, ROWS, WIDTH), BF16),
            pltpu.VMEM((chunks, ROWS + STATS, WIDTH), BF16),
            pltpu.VMEM((ROWS, 5 * ROWS), F32),
            pltpu.VMEM((ROWS, 2 * TAPS), F32),
            pltpu.VMEM((ROWS, LANES), F32),
            pltpu.VMEM((filters.shape[0], 2 * TAPS), F32),
            pltpu.VMEM((width // LANES, ROWS, LANES // GROUP * 2 * TAPS), BF16),
            many,
            many,
            some,
            some,
            many,
            many,
            some,
            some,
            some,
            some,
            some,
            few,
            few,
            few,
            few,
        ],
        compiler_params=pltpu.CompilerParams(
            collective_id=0, has_side_effects=True, vmem_limit_bytes=56 * 2**20
        ),
        name="layer",
    )(
        lengths.reshape(1, -1),
        queries,
        key_rows,
        value_rows,
        norm_gain.reshape(1, -1),
        filters,
        bypass.reshape(1, -1),
    )


def solution(mesh):
    rows = P(("dp", "ctx"), None)
    return jax.shard_map(
        functools.partial(shards, mesh),
        mesh=mesh,
        in_specs=(rows, rows, rows, P("dp"), P(), P(), P()),
        out_specs=rows,
        check_vma=False,
    )
```
